128 devices in a mesh: body: 2 (over y_lo), row: 8 (over y_hi, x), col: 8 (over z, core).
Axes of the slice: x: 4, y: 4 (y_hi: 2, y_lo: 2; y = y_hi * 2 + y_lo), z: 4, core: 2. Of those that a mesh axis runs over, the one named last changes fastest.
Arguments:
- lam_start: float32 [2, 128, 16384], P('body', None, ('row', 'col')), may hold values from -8 to 8
- load: float32 [2, 128, 16384], P('body', None, ('row', 'col')), may hold values from -24 to 24
- operator: bfloat16 [2, 16384, 8, 8, 256], P('body', 'row', None, 'col'), as said below
- partner: int32 [2, 16384], P('body', ('row', 'col')), may hold values from 0 to 16383, as said below
- active: int32 [16384], P(('row', 'col')), may hold values 0 or 1
- bounds: int32 [2, 2], P('body'), may hold values from 1 to 20, as said below
Outputs:
- multipliers: float32 [2, 128, 16384], P('body', None, ('row', 'col'))
- residual: float32 [2, 128, 16384], P('body', None, ('row', 'col'))
The draws below stay inside these ranges and needn't reach their ends.
Inputs may be any that keep to these rules, and one draw needn't show every extreme that they name: Each operator F_b is symmetric, with positive diagonal. partner[0] maps every aligned block of 256 unknowns onto itself, one to one, and partner[1] is its inverse: partner[1, partner[0, i]] = i. bounds[b, 0] is 1 or 2 and bounds[b, 1] is 18 to 20.
All inputs are finite; a program needn't handle non-finite values. No bound on the sum of `active` on one device may be relied on, other than what follows from the above.
Results may differ from the reference program's by a relative error of at most 0.03.
The reference program's roundings to bfloat16 on the way count: a program that leaves them out, or rounds other values in their place, can miss the bound.
Values may be sent and summed in bfloat16 or wider, within the bound.
No kernel may reach another device: no remote copies, remote signals or barrier semaphores. Data moves between devices by JAX's collectives and lax.ppermute only.
A program may use at most 64 MiB of HBM per device.

```python
import jax
import jax.numpy as jnp
from jax import lax

M = 16384
R = 128
K = 4
PIECE = 256
BODIES = 2
N_ROW = 8
N_COL = 8


def draw_operator(key, part):
    keys = jax.random.split(jax.random.fold_in(key, 11), 2)

    def single(subkey):
        first_key, second_key = jax.random.split(subkey, 2)
        noise = jax.random.normal(first_key, (M, M), jnp.float32)
        sym = (noise + noise.T) * (1.4142135 / jnp.sqrt(jnp.float32(M)))
        diag_vals = jax.random.uniform(second_key, (M,), jnp.float32, 6.0, 14.0)
        idx = jnp.arange(M)
        sym = sym.at[idx, idx].add(diag_vals)
        return sym.astype(jnp.bfloat16)
    return lax.map(single, keys).reshape(2, M, N_ROW, N_COL, PIECE)


def draw_partner(key, part):
    blocks = M // PIECE
    keys = jax.random.split(jax.random.fold_in(key, 23), blocks)
    perms = jax.vmap(lambda subkey: jax.random.permutation(subkey, PIECE))(keys).astype(jnp.int32)
    offsets = (jnp.arange(blocks, dtype=jnp.int32) * PIECE)[:, None]
    forward = (perms + offsets).reshape(M)
    inverse = jnp.argsort(forward, stable=True).astype(jnp.int32)
    return jnp.stack([forward, inverse])


def draw_bounds(key, part):
    first_key, second_key = jax.random.split(jax.random.fold_in(key, 37))
    lower = jax.random.randint(first_key, (2,), 1, 3, jnp.int32)
    upper = jax.random.randint(second_key, (2,), 18, 21, jnp.int32)
    return jnp.stack([lower, upper], axis=1)


def touch_ends(drawn, key, smallest, high):
    extent = drawn.shape
    place = [jax.random.randint(jax.random.fold_in(key, axis), (), 0, extent[axis]) for axis in range(len(extent))]
    drawn = drawn.at[tuple(place)].set(smallest)
    longest = extent.index(max(extent))
    place[longest] = (place[longest] + 1) % extent[longest]
    return drawn.at[tuple(place)].set(high)


def block_levels(own_key, dims, shards, low, high):
    factor_of, own = 1.0, jax.random.fold_in(own_key, 6)
    for axis_at, shards_of in shards:
        steps = jnp.exp(jax.random.uniform(jax.random.fold_in(own, axis_at), (shards_of,), jnp.float32, low / len(shards), high / len(shards)))
        factor_of = factor_of * jnp.repeat(steps, dims[axis_at] // shards_of).reshape([-1 if axis == axis_at else 1 for axis in range(len(dims))])
    return factor_of


def normal_values(stream_key, shape, width, limit, cuts=(), held_as=jnp.bfloat16):
    values = jax.random.normal(stream_key, shape, jnp.float32) * width
    if len(cuts) > 0:
        values = block_levels(stream_key, shape, cuts, -0.22, 0.18) * values
    return jnp.clip(values, min=-limit, max=limit).astype(held_as)


def setup_inputs(seed: int = 0) -> dict:
    seeds = jax.random.split(jax.random.key(seed), 7)
    return {
        "lam_start": normal_values(seeds[0], (BODIES, R, M), 3.0, 8.0, ((0, 2), (2, 64)), jnp.float32),
        "load": normal_values(seeds[1], (BODIES, R, M), 4.0, 24.0, ((0, 2), (2, 64)), jnp.float32),
        "operator": draw_operator(jax.random.fold_in(seeds[6], 71), 0),
        "partner": draw_partner(jax.random.fold_in(seeds[6], 71), 0),
        "active": touch_ends((jax.random.randint(seeds[4], (M,), 0, 2) < 1).astype(jnp.int32), jax.random.fold_in(seeds[4], 1), 0, 1),
        "bounds": draw_bounds(jax.random.fold_in(seeds[6], 71), 0),
    }


def apply_all(field, dense):
    rounded = field.astype(jnp.bfloat16)
    outs = []
    for which in range(2):
        outs.append(lax.dot_general(rounded[which], dense[which], (((1,), (1,)), ((), ())), preferred_element_type=jnp.float32))
    return jnp.stack(outs)


def clamp_all(lam, partner, active):
    mate = jnp.stack([jnp.take(lam[1], partner[0], axis=1), jnp.take(lam[0], partner[1], axis=1)])
    flags = jnp.stack([active, jnp.take(active, partner[1])]) > 0
    sign = jnp.array([1.0, -1.0], jnp.float32)[:, None, None]
    middle = 0.5 * (lam + mate)
    normal = 0.5 * sign * (lam - mate)
    normal = jnp.where(flags[:, None, :], jnp.maximum(normal, 0.0), normal)
    return middle + sign * normal


def cheb_pass(start, load, dense, bounds):
    lower = bounds[:, 0].astype(jnp.float32)[:, None, None]
    upper = bounds[:, 1].astype(jnp.float32)[:, None, None]
    theta = 0.5 * (upper + lower)
    delta = 0.5 * (upper - lower)
    sigma = theta / delta
    answer = start
    resid = load - apply_all(answer, dense)
    direction = resid / theta
    rho = delta / theta
    for step in range(K):
        answer = answer + direction
        resid = resid - apply_all(direction, dense)
        if step + 1 < K:
            rho_new = 1.0 / (2.0 * sigma - rho)
            direction = rho_new * rho * direction + (2.0 * rho_new / delta) * resid
            rho = rho_new
    return answer, resid


def reference(lam_start, load, operator, partner, active, bounds):
    dense = operator.reshape(2, M, M)
    first = clamp_all(lam_start, partner, active)
    second, unused = cheb_pass(first, load, dense, bounds)
    third = clamp_all(second, partner, active)
    return cheb_pass(third, load, dense, bounds)
```

```python
import functools

import jax
import jax.numpy as jnp
from jax import lax
from jax.experimental import pallas as pl
from jax.experimental.pallas import tpu as pltpu
from jax.sharding import PartitionSpec as P

K = 4
X = 4
Z = 4


def permute(value, axis, target):
    pairs = [(source, target(source)) for source in range(lax.axis_size(axis))]
    return lax.ppermute(value, axis, pairs)


def across_body(value):
    return permute(value, "body", lambda s: s ^ 1)


def across_core(value):
    return permute(value, "col", lambda s: s ^ 1)


def across_y(value):
    return permute(value, "row", lambda s: s ^ X)


def along_x(value, step):
    return permute(value, "row", lambda s: s // X * X + (s % X + step) % X)


def along_z(value, step):
    return permute(value, "col", lambda s: (s // 2 + step) % Z * 2 + s % 2)


def product_kernel(other, tile_ref, v0_ref, v1_ref, v2_ref, v3_ref, out_ref, field_ref):
    row = lax.axis_index("row")
    col = lax.axis_index("col")
    piece = out_ref.shape[1]
    high, x = row // X, row % X
    z, core = col // 2, col % 2
    for step, v_ref in enumerate((v0_ref, v1_ref, v2_ref, v3_ref)):
        source = (x + X - step) % X
        for which, side in ((0, high), (1, 1 - high)):
            start = pl.multiple_of((side * X + source) * piece, piece)
            field_ref[pl.ds(start, piece), :] = v_ref[which]
    lane = 1 - core if other else core
    for step in range(Z):
        start = pl.multiple_of(((z + step) % Z * 2 + lane) * piece, piece)
        out_ref[step] = jnp.dot(
            tile_ref[pl.ds(start, piece), :], field_ref[...], preferred_element_type=jnp.float32
        )


def product(tile, parts, other):
    two, piece, loads = parts[0].shape
    rows, width = tile.shape
    spec = pl.BlockSpec(memory_space=pltpu.VMEM)
    return pl.pallas_call(
        functools.partial(product_kernel, other),
        out_shape=jax.ShapeDtypeStruct((Z, piece, loads), jnp.float32),
        in_specs=[spec] * 5,
        out_specs=spec,
        scratch_shapes=[pltpu.VMEM((width, loads), jnp.bfloat16)],
        compiler_params=pltpu.CompilerParams(vmem_limit_bytes=8 << 20),
        cost_estimate=pl.CostEstimate(
            flops=rows * width * loads, bytes_accessed=rows * width, transcendentals=0
        ),
        name="product_other" if other else "product_own",
    )(tile, *parts)


def apply_tile(field, tile):
    rounded = field.astype(jnp.bfloat16)
    both = jnp.stack([rounded, across_y(rounded)])
    parts = [both] + [along_x(both, step) for step in (1, 2, 3)]
    given = across_core(product(tile, parts, True))
    kept = product(tile, parts, False)
    sums = [kept[step] + given[step] for step in range(Z)]
    moved = [along_z(sums[step], step) for step in (2, 1, 3)]
    return (sums[0] + moved[1]) + (moved[0] + moved[2])


def clamp_local(lam, local, flags, sign):
    mate = jnp.take(across_body(lam), local, axis=0)
    middle = 0.5 * (lam + mate)
    normal = 0.5 * sign * (lam - mate)
    normal = jnp.where(flags, jnp.maximum(normal, 0.0), normal)
    return middle + sign * normal


def cheb_local(start, load, tile, lower, upper):
    theta = 0.5 * (upper + lower)
    delta = 0.5 * (upper - lower)
    sigma = theta / delta
    answer = start
    resid = load - apply_tile(answer, tile)
    direction = resid / theta
    rho = delta / theta
    for step in range(K):
        answer = answer + direction
        resid = resid - apply_tile(direction, tile)
        if step + 1 < K:
            rho_new = 1.0 / (2.0 * sigma - rho)
            direction = rho_new * rho * direction + 2.0 * rho_new / delta * resid
            rho = rho_new
    return (answer, resid)


def per_device(lam_start, load, operator, partner, active, bounds):
    tile = operator.reshape(operator.shape[1], operator.shape[2] * operator.shape[4])
    lower = bounds[0, 0].astype(jnp.float32)
    upper = bounds[0, 1].astype(jnp.float32)
    width = lam_start.shape[2]
    own_load = load[0].T
    local = partner[0] % width
    which = lax.axis_index("body")
    sign = (1 - 2 * which).astype(jnp.float32)
    flag_index = jnp.where(which == 0, jnp.arange(width, dtype=jnp.int32), local)
    flags = (jnp.take(active, flag_index) > 0)[:, None]
    first = clamp_local(lam_start[0].T, local, flags, sign)
    second, unused = cheb_local(first, own_load, tile, lower, upper)
    third = clamp_local(second, local, flags, sign)
    answer, resid = cheb_local(third, own_load, tile, lower, upper)
    return (answer.T[None], resid.T[None])


def solution(mesh):
    return jax.shard_map(
        per_device,
        mesh=mesh,
        in_specs=(
            P("body", None, ("row", "col")),
            P("body", None, ("row", "col")),
            P("body", "row", None, "col", None),
            P("body", ("row", "col")),
            P(("row", "col")),
            P("body", None),
        ),
        out_specs=(P("body", None, ("row", "col")), P("body", None, ("row", "col"))),
        check_vma=False,
    )
```

```python
import functools

import jax
import jax.numpy as jnp
from jax import lax
from jax.experimental import pallas as pl
from jax.experimental.pallas import tpu as pltpu
from jax.sharding import PartitionSpec as P

K = 4
X = 4
Z = 4
LANES = 128
FLIPS = (0, 1, 3, 2)


IN_VMEM = pl.BlockSpec(memory_space=pltpu.VMEM)
IN_SMEM = pl.BlockSpec(memory_space=pltpu.SMEM)
IN_PLACE = pl.BlockSpec(memory_space=pl.ANY)


def permute(value, axis, mask):
    pairs = [(source, source ^ mask) for source in range(lax.axis_size(axis))]
    return lax.ppermute(value, axis, pairs)


def held(*values):
    return [pltpu.with_memory_space_constraint(value, pltpu.VMEM) for value in values]


def gray(value):
    return value ^ (value >> 1)


def arrange_kernel(tile_ref, out_ref, slot_ref, wide_ref, sem):
    row = lax.axis_index("row")
    col = lax.axis_index("col")
    groups = 2 * X
    rows, piece = slot_ref.shape[1:]
    blocks = out_ref.shape[0] // piece

    def fetch(block, slot):
        target = col ^ (1 - block // Z) ^ (2 * gray(block % Z))
        start = pl.multiple_of(target * rows, rows)
        return pltpu.make_async_copy(
            tile_ref.at[pl.ds(start, rows), :], slot_ref.at[slot], sem.at[slot]
        )

    fetch(0, 0).start()

    @pl.loop(0, blocks)
    def _(block):
        slot = block % 2

        @pl.when(block + 1 < blocks)
        def _():
            fetch(block + 1, 1 - slot).start()

        fetch(block, slot).wait()

        @pl.loop(0, groups)
        def _(part):
            place = pl.ds(pl.multiple_of(part * piece, piece), piece)
            wide = slot_ref[slot, place, :].astype(jnp.float32)
            for lane in range(2):
                wide_ref[lane, place, :] = wide[:, lane * LANES : (lane + 1) * LANES]

        @pl.loop(0, groups)
        def _(source):
            turn = source ^ row
            place = pl.multiple_of((gray(turn % X) * 2 + turn // X) * piece, piece)
            below = pl.ds(pl.multiple_of(block * piece, piece), piece)
            for lane in range(2):
                beside = pl.ds(pl.multiple_of(place + lane * LANES, LANES), LANES)
                out_ref[below, beside] = wide_ref[
                    lane, pl.ds(source, piece, stride=groups), :
                ].astype(jnp.bfloat16)


def arrange(operator):
    rows, groups, piece = operator.shape[1], operator.shape[2], operator.shape[4]
    return pl.pallas_call(
        arrange_kernel,
        out_shape=pltpu.VMEM((rows, groups * piece), operator.dtype),
        in_specs=[IN_PLACE],
        out_specs=IN_VMEM,
        scratch_shapes=[
            pltpu.VMEM((2, groups * piece, piece), operator.dtype),
            pltpu.VMEM((2, groups * piece, LANES), jnp.float32),
            pltpu.SemaphoreType.DMA((2,)),
        ],
        compiler_params=pltpu.CompilerParams(vmem_limit_bytes=6 << 20),
        cost_estimate=pl.CostEstimate(
            flops=0, bytes_accessed=8 * rows * groups * piece, transcendentals=0
        ),
        name="arrange",
    )(operator.reshape(rows * groups, piece))


def early_kernel(tile_ref, v0_ref, v1_ref, out_ref):
    rows = out_ref.shape[0]
    width = v0_ref.shape[0]

    @pl.loop(0, rows // 512)
    def _(step):
        place = pl.ds(pl.multiple_of(step * 512, 512), 512)
        out_ref[place, :] = jnp.dot(
            tile_ref[place, :width], v0_ref[...], preferred_element_type=jnp.float32
        ) + jnp.dot(
            tile_ref[place, width : 2 * width], v1_ref[...], preferred_element_type=jnp.float32
        )


def later_kernel(first, order, tile_ref, total_ref, v_ref, out_ref):
    rows = out_ref.shape[0]
    width = v_ref.shape[0]
    step_rows = min(rows, 1024)

    @pl.loop(0, rows // step_rows)
    def _(step):
        start = pl.multiple_of(step * step_rows, step_rows)
        place = pl.ds(start + first, step_rows)
        out_ref[pl.ds(start, step_rows), :] = total_ref[place, :] + jnp.dot(
            tile_ref[place, order * width : (order + 1) * width],
            v_ref[...],
            preferred_element_type=jnp.float32,
        )


def estimate(rows, width, loads):
    return pl.CostEstimate(
        flops=2 * rows * width * loads, bytes_accessed=2 * rows * width, transcendentals=0
    )


def early(tile, v0, v1):
    rows = tile.shape[0]
    width, loads = v0.shape
    return pl.pallas_call(
        early_kernel,
        out_shape=pltpu.VMEM((rows, loads), jnp.float32),
        in_specs=[IN_VMEM] * 3,
        out_specs=IN_VMEM,
        compiler_params=pltpu.CompilerParams(vmem_limit_bytes=4 << 20),
        cost_estimate=estimate(rows, 2 * width, loads),
        name="early",
    )(*held(tile, v0, v1))


def later(tile, total, v, order, first, rows):
    width, loads = v.shape
    return pl.pallas_call(
        functools.partial(later_kernel, first, order),
        out_shape=pltpu.VMEM((rows, loads), jnp.float32),
        in_specs=[IN_VMEM] * 3,
        out_specs=IN_VMEM,
        compiler_params=pltpu.CompilerParams(vmem_limit_bytes=4 << 20),
        cost_estimate=estimate(rows, width, loads),
        name=f"later_{order}_{first}",
    )(*held(tile, total, v))


def summed(field, tile):
    piece, loads = field.shape
    both = jnp.concatenate([field, permute(field, "row", X)])
    parts = [permute(both, "row", turn) for turn in FLIPS[1:]]
    total = early(tile, both, parts[0])
    total = later(tile, total, parts[1], 2, 0, tile.shape[0])
    half = tile.shape[0] // 2
    given = permute(later(tile, total, parts[2], 3, 0, half), "col", 1)
    kept = later(tile, total, parts[2], 3, half, half)
    sums = (kept + given).reshape(Z, piece, loads)
    return [sums[0]] + [permute(sums[n], "col", 2 * FLIPS[n]) for n in range(1, Z)]


def coefficients(lower, upper):
    theta = 0.5 * (upper + lower)
    delta = 0.5 * (upper - lower)
    sigma = theta / delta
    rho = delta / theta
    coefs = [(None, 1.0 / theta)]
    for step in range(K - 1):
        rho_new = 1.0 / (2.0 * sigma - rho)
        coefs.append((rho_new * rho, 2.0 * rho_new / delta))
        rho = rho_new
    return coefs


def cheb_local(start, rounded, load, tile, coefs, steps):
    answer, resid, direction = None, load, start
    for step in range(steps):
        answer = direction if answer is None else answer + direction
        sums = summed(rounded, tile)
        resid = resid - ((sums[0] + sums[1]) + (sums[2] + sums[3]))
        if step < K:
            kept, gained = coefs[step]
            direction = gained * resid if kept is None else kept * direction + gained * resid
            rounded = direction.astype(jnp.bfloat16)
    return answer, resid, direction


def clamp_kernel(turned, lam_ref, peer_ref, local_ref, active_ref, out_ref, round_ref, peer_scr, mate_scr, flag_scr):
    body = lax.axis_index("body")
    piece, loads = out_ref.shape
    peer_scr[...] = peer_ref[...] if turned else peer_ref[...].T
    lam = lam_ref[...] if turned else lam_ref[...].T

    @pl.loop(0, piece, unroll=8)
    def _(place):
        local = local_ref[place] % piece
        flag = active_ref[jnp.where(body == 0, place, local)]
        mate_scr[pl.ds(place, 1), :] = peer_scr[pl.ds(local, 1), :]
        flag_scr[pl.ds(place, 1), :] = jnp.full((1, loads), flag, jnp.int32)

    mate = mate_scr[...]
    sign = (1 - 2 * body).astype(jnp.float32)
    middle = 0.5 * (lam + mate)
    normal = 0.5 * sign * (lam - mate)
    normal = jnp.where(flag_scr[...] > 0, jnp.maximum(normal, 0.0), normal)
    result = middle + sign * normal
    out_ref[...] = result
    round_ref[...] = result.astype(jnp.bfloat16)


def clamp_local(turned, lam, local, active):
    shape = lam.shape if turned else lam.shape[::-1]
    return pl.pallas_call(
        functools.partial(clamp_kernel, turned),
        out_shape=[pltpu.VMEM(shape, jnp.float32), pltpu.VMEM(shape, jnp.bfloat16)],
        in_specs=[IN_VMEM, IN_VMEM, IN_SMEM, IN_SMEM],
        out_specs=[IN_VMEM] * 2,
        scratch_shapes=[
            pltpu.VMEM(shape, jnp.float32),
            pltpu.VMEM(shape, jnp.float32),
            pltpu.VMEM(shape, jnp.int32),
        ],
        compiler_params=pltpu.CompilerParams(vmem_limit_bytes=4 << 20),
        name="clamp_turned" if turned else "clamp",
    )(lam, permute(lam, "body", 1), local, active)


def per_device(lam_start, load, operator, partner, active, bounds):
    coefs = coefficients(bounds[0, 0].astype(jnp.float32), bounds[0, 1].astype(jnp.float32))
    own_load = load[0].T
    local = partner[0]
    first, rounded = clamp_local(False, lam_start[0], local, active)
    operator, coefs, own_load = lax.optimization_barrier((operator, coefs, own_load))
    tile = arrange(operator)
    answer, unused, direction = cheb_local(first, rounded, own_load, tile, coefs, K)
    third, rounded = clamp_local(True, answer + direction, local, active)
    answer, resid, unused = cheb_local(third, rounded, own_load, tile, coefs, K + 1)
    return (answer.T[None], resid.T[None])


def solution(mesh):
    return jax.shard_map(
        per_device,
        mesh=mesh,
        in_specs=(
            P("body", None, ("row", "col")),
            P("body", None, ("row", "col")),
            P("body", "row", None, "col", None),
            P("body", ("row", "col")),
            P(("row", "col")),
            P("body", None),
        ),
        out_specs=(P("body", None, ("row", "col")), P("body", None, ("row", "col"))),
        check_vma=False,
    )
```
